32 devices in a mesh: ia: 8 (over y, x, core), ja: 4 (over z).
Axes of the slice: x: 2, y: 2, z: 4, core: 2. Of those that a mesh axis runs over, the one named last changes fastest.
Arguments:
- slabs: bfloat16 [32, 512, 512], P(('ia', 'ja')), may hold values from -1.1953125 to 1.1953125
- pno_coef: bfloat16 [512, 256, 128], P(('ia', 'ja')), may hold values from -0.375 to 0.375
- dom_blocks: int32 [512, 2], P(('ia', 'ja')), may hold values from 0 to 3, as said below
- pair_first: int32 [512], P(('ia', 'ja')), may hold values from 0 to 3
- pair_second: int32 [512], P(('ia', 'ja')), may hold values from 0 to 7
- pno_energy: float32 [512, 128], P(('ia', 'ja')), may hold values from 0.3 to 3
- pair_shift: float32 [512], P(('ia', 'ja')), may hold values from 0.5 to 2
- margin_i: bfloat16 [512, 16, 128, 128], P(('ia', 'ja')), may hold values from -0.5 to 0.5
- margin_j: bfloat16 [512, 16, 128, 128], P(('ia', 'ja')), may hold values from -0.5 to 0.5
- couple_i: float32 [512, 16], P(('ia', 'ja')), may hold values from -0.45 to 0.45
- couple_j: float32 [512, 16], P(('ia', 'ja')), may hold values from -0.45 to 0.45
- ask_i: int32 [32, 8, 4], P(('ia', 'ja')), may hold values from 0 to 15, as said below
- ask_j: int32 [32, 4, 4], P(('ia', 'ja')), may hold values from 0 to 15, as said below
- link_i: int32 [512, 16], P(('ia', 'ja')), may hold values from 0 to 31, as said below
- link_j: int32 [512, 16], P(('ia', 'ja')), may hold values from 0 to 15, as said below
Outputs:
- amplitudes: float32 [512, 128, 128], P(('ia', 'ja'))
- density: float32 [512, 512], P(('ia', 'ja'))
The draws below stay inside these ranges and needn't reach their ends.
Inputs may be any that keep to these rules, and one draw needn't show every extreme that they name: `dom_blocks`: the 2 blocks of a pair are distinct. `ask_i`: for each block g and each peer s, the 4 slots are distinct. `ask_j`: for each block g and each peer s, the 4 slots are distinct. `link_i`: within each aligned block of 16 pairs every value is named at least once. `link_j`: within each aligned block of 16 pairs every value is named at least once.
All inputs are finite; a program needn't handle non-finite values.
Results may differ from the reference program's by a relative error of at most 0.0045.
Values may be sent and summed in bfloat16 or wider, within the bound.
A program may use at most 128 MiB of HBM per device.

```python
import math
import jax
import jax.numpy as jnp
from jax import lax

NPNO = 128
PAO = 512
AUX = 512
BLK = 128
DOMB = 2
NB_I = 16
NB_J = 16
ITERS = 2
PAIR_DEV = 16
NBLK = 4
DOM = 256
CAP_I = 4
CAP_J = 4
BLOCKS = 32
PAIRS = 512
NOCC = 32
I_SPAN = 4
J_SPAN = 8
ROW_TABLE = 32
COL_TABLE = 16
N_IA = 8
N_JA = 4


def distinct_first(key, shape, pool_size, taken):
    scores = jax.random.randint(key, shape + (pool_size,), 0, 1 << 20) * pool_size + jnp.arange(pool_size, dtype=jnp.int32)
    ranking = jnp.argsort(scores, axis=-1, stable=True)
    return ranking[..., :taken].astype(jnp.int32)


def spread_links(key, table_size, per_block):

    def single(subkey):
        filler = jax.random.randint(subkey, (per_block - table_size,), 0, table_size).astype(jnp.int32)
        values = jnp.concatenate([jnp.arange(table_size, dtype=jnp.int32), filler])
        return jax.random.permutation(jax.random.fold_in(subkey, 7), values)
    return jax.vmap(single)(jax.random.split(key, BLOCKS))


def draw_dom_blocks(key, part):
    return distinct_first(jax.random.fold_in(key, 3), (PAIRS,), NBLK, DOMB)


def draw_ask_i(key, part):
    return distinct_first(jax.random.fold_in(key, 5), (BLOCKS, N_IA), PAIR_DEV, CAP_I)


def draw_ask_j(key, part):
    return distinct_first(jax.random.fold_in(key, 9), (BLOCKS, N_JA), PAIR_DEV, CAP_J)


def draw_link_i(key, part):
    return spread_links(jax.random.fold_in(key, 11), ROW_TABLE, PAIR_DEV * NB_I).reshape(PAIRS, NB_I)


def draw_link_j(key, part):
    return spread_links(jax.random.fold_in(key, 13), COL_TABLE, PAIR_DEV * NB_J).reshape(PAIRS, NB_J)


def set_ends(values, key, least, largest):
    longest = values.shape.index(max(values.shape))
    spots = []
    for shift in (0, 1):
        where = [jax.random.randint(jax.random.fold_in(key, axis), (), 0, length) for axis, length in enumerate(values.shape)]
        where[longest] = (where[longest] + shift) % values.shape[longest]
        spots.append(tuple(where))
    return values.at[spots[0]].set(least).at[spots[1]].set(largest)


def levels(rng, extent, cuts, least, high):
    factor_of = 1.0
    for axis_at, shards_of in cuts:
        heights = jax.random.uniform(jax.random.fold_in(jax.random.fold_in(rng, 6), axis_at), (shards_of,), jnp.float32, least / len(cuts), high / len(cuts))
        factor_of = factor_of * jnp.repeat(jnp.exp(heights), extent[axis_at] // shards_of).reshape((-1,) + (1,) * (len(extent) - 1 - axis_at))
    return factor_of


def gaussian(stream_key, dims, deviation, reach, shards=(), kind=jnp.bfloat16):
    values = jax.random.normal(stream_key, dims, jnp.float32) * deviation
    if len(shards) > 0:
        values = levels(stream_key, dims, shards, -0.22, 0.18) * values
    return jnp.clip(values, min=-reach, max=reach).astype(kind)


def setup_inputs(seed: int = 0) -> dict:
    streams_of = jax.random.split(jax.random.key(seed), 16)
    slabs = gaussian(streams_of[0], (NOCC, PAO, AUX), 0.2, 1.1953125, ((0, 32),))
    pno_coef = gaussian(streams_of[1], (PAIRS, DOM, NPNO), DOM ** -0.5, 0.375, ((0, 32),))
    dom_blocks = draw_dom_blocks(jax.random.fold_in(streams_of[15], 71), 0)
    pair_first = set_ends(jax.random.randint(streams_of[3], (PAIRS,), 0, I_SPAN), jax.random.fold_in(streams_of[3], 1), 0, I_SPAN - 1).astype(jnp.int32)
    pair_second = set_ends(jax.random.randint(streams_of[4], (PAIRS,), 0, J_SPAN), jax.random.fold_in(streams_of[4], 1), 0, J_SPAN - 1).astype(jnp.int32)
    pno_energy = jnp.clip(jnp.exp(math.log(3.0) - 2.3025851 * jax.random.uniform(streams_of[5], (PAIRS, NPNO), jnp.float32) ** levels(streams_of[5], (PAIRS, NPNO), ((0, 32),), -0.2, 0.2)), 0.3, 3.0)
    pair_shift = jnp.clip(jnp.exp(math.log(2.0) - 1.3862944 * jax.random.uniform(streams_of[6], (PAIRS,), jnp.float32) ** levels(streams_of[6], (PAIRS,), ((0, 32),), -0.2, 0.2)), 0.5, 2.0)
    margin_i = gaussian(streams_of[7], (PAIRS, NB_I, NPNO, NPNO), NPNO ** -0.5, 0.5, ((0, 32),))
    margin_j = gaussian(streams_of[8], (PAIRS, NB_J, NPNO, NPNO), NPNO ** -0.5, 0.5, ((0, 32),))
    couple_i = jnp.clip(jax.random.uniform(streams_of[9], (PAIRS, NB_I), jnp.float32, -0.45, 0.45) * levels(streams_of[9], (PAIRS, NB_I), ((0, 32),), -0.4, 0.0), -0.45, 0.45)
    couple_j = jnp.clip(jax.random.uniform(streams_of[10], (PAIRS, NB_J), jnp.float32, -0.45, 0.45) * levels(streams_of[10], (PAIRS, NB_J), ((0, 32),), -0.4, 0.0), -0.45, 0.45)
    ask_i = draw_ask_i(jax.random.fold_in(streams_of[15], 71), 0)
    ask_j = draw_ask_j(jax.random.fold_in(streams_of[15], 71), 0)
    link_i = draw_link_i(jax.random.fold_in(streams_of[15], 71), 0)
    link_j = draw_link_j(jax.random.fold_in(streams_of[15], 71), 0)
    return dict(slabs=slabs, pno_coef=pno_coef, dom_blocks=dom_blocks, pair_first=pair_first, pair_second=pair_second, pno_energy=pno_energy, pair_shift=pair_shift, margin_i=margin_i, margin_j=margin_j, couple_i=couple_i, couple_j=couple_j, ask_i=ask_i, ask_j=ask_j, link_i=link_i, link_j=link_j)


def coupled(near_blocks, margin_blocks, weights):
    left_side = jnp.einsum('nab,nbc->nac', margin_blocks.astype(jnp.float32), near_blocks.astype(jnp.float32)).astype(jnp.bfloat16)
    product = jnp.einsum('nac,ndc->nad', left_side.astype(jnp.float32), margin_blocks.astype(jnp.float32))
    return lax.optimization_barrier(jnp.sum(weights[:, None, None] * product, axis=0))

def reference(slabs, pno_coef, dom_blocks, pair_first, pair_second, pno_energy, pair_shift, margin_i, margin_j, couple_i, couple_j, ask_i, ask_j, link_i, link_j):
    pair_index = jnp.arange(PAIRS, dtype=jnp.int32)
    owner_block = pair_index // PAIR_DEV
    block_row = owner_block // N_JA
    block_col = owner_block % N_JA
    first_orbital = block_row * N_JA + pair_first
    second_orbital = pair_second * N_JA + block_col
    slab_blocks = slabs.reshape(NOCC * NBLK, BLK, AUX)

    def pair_exchange(packed):
        orbital_one, orbital_two, coefs, domains = packed
        rows_one = slab_blocks[orbital_one * NBLK + domains].reshape(DOM, AUX)
        rows_two = slab_blocks[orbital_two * NBLK + domains].reshape(DOM, AUX)
        projected_one = jnp.dot(coefs.T, rows_one, preferred_element_type=jnp.float32).astype(jnp.bfloat16)
        projected_two = jnp.dot(coefs.T, rows_two, preferred_element_type=jnp.float32).astype(jnp.bfloat16)
        return jnp.dot(projected_one, projected_two.T, preferred_element_type=jnp.float32)
    exchange_ints = lax.map(pair_exchange, (first_orbital, second_orbital, pno_coef, dom_blocks))
    denominator = pno_energy[:, :, None] + pno_energy[:, None, :] + pair_shift[:, None, None]
    amplitudes = -exchange_ints / denominator
    peer_first = link_i // CAP_I
    slot_first = link_i % CAP_I
    near_first = (peer_first * N_JA + block_col[:, None]) * PAIR_DEV + ask_i[owner_block[:, None], peer_first, slot_first]
    peer_second = link_j // CAP_J
    slot_second = link_j % CAP_J
    near_second = (block_row[:, None] * N_JA + peer_second) * PAIR_DEV + ask_j[owner_block[:, None], peer_second, slot_second]
    for iteration in range(ITERS):
        sent = amplitudes.astype(jnp.bfloat16)

        def pair_coupling(packed):
            index_one, margin_one, weight_one, index_two, margin_two, weight_two = packed
            return coupled(sent[index_one], margin_one, weight_one) + coupled(sent[index_two], margin_two, weight_two)
        coupling = lax.map(pair_coupling, (near_first, margin_i, couple_i, near_second, margin_j, couple_j))
        residual = exchange_ints + denominator * amplitudes + coupling
        amplitudes = amplitudes - residual / denominator
    sent = amplitudes.astype(jnp.bfloat16)

    def accumulate(running, packed):
        amp_block, coefs, domains = packed
        square = (jnp.dot(amp_block, amp_block.T, preferred_element_type=jnp.float32) + jnp.dot(amp_block.T, amp_block, preferred_element_type=jnp.float32)).astype(jnp.bfloat16)
        mapped = jnp.dot(coefs, square, preferred_element_type=jnp.float32).astype(jnp.bfloat16)
        domain_density = jnp.dot(mapped, coefs.T, preferred_element_type=jnp.float32)
        select = (domains[:, None] == jnp.arange(NBLK, dtype=jnp.int32)[None, :]).astype(jnp.float32)
        placed = jnp.einsum('kg,lh,krlc->grhc', select, select, domain_density.reshape(DOMB, BLK, DOMB, BLK), precision=lax.Precision.HIGHEST)
        return (running + placed.reshape(PAO, PAO), None)
    running, unused = lax.scan(accumulate, jnp.zeros((PAO, PAO), jnp.float32), (sent, pno_coef, dom_blocks))
    density = running * (1.0 / math.sqrt(PAIRS))
    return (amplitudes, density)
```

```python
import functools
import math

import jax
import jax.numpy as jnp
from jax import lax
from jax.experimental import pallas as pl
from jax.experimental.pallas import tpu as pltpu
from jax.sharding import PartitionSpec as P

BLK = 128
ITERS = 2
MESH = pl.DeviceIdType.MESH
F32 = jnp.float32
BF16 = jnp.bfloat16


def matmul(a, b, da, db):
    return lax.dot_general(a, b, (((da,), (db,)), ((), ())), preferred_element_type=F32)


def enter(n_ia, n_ja, ia, ja):
    barrier = pltpu.get_barrier_semaphore()
    for k in range(1, n_ia):
        pl.semaphore_signal(
            barrier, inc=1, device_id=(lax.rem(ia + k, n_ia), ja), device_id_type=MESH
        )
    for k in range(1, n_ja):
        pl.semaphore_signal(
            barrier, inc=1, device_id=(ia, lax.rem(ja + k, n_ja)), device_id_type=MESH
        )
    pl.semaphore_wait(barrier, n_ia + n_ja - 2)


def remote(src, dst, send, recv, device):
    return pltpu.make_async_remote_copy(
        src_ref=src, dst_ref=dst, send_sem=send, recv_sem=recv, device_id=device,
        device_id_type=MESH,
    )


def exchange_kernel(
    n_ia, n_ja,
    slabs, ask_i, ask_j, coef, dom, first, second,
    exch, all_i, all_j,
    row_slabs, col_slabs,
    loc, row_s, row_r, col_s, col_r, fwd_s, fwd_r, ai_s, ai_r, aj_s, aj_r,
):
    ia, ja = lax.axis_index("ia"), lax.axis_index("ja")
    half = n_ia // 2
    partner = ia + 1 - 2 * lax.rem(ia, 2)
    locals_ = [
        pltpu.make_async_copy(slabs, row_slabs.at[ja], loc.at[0]),
        pltpu.make_async_copy(slabs, col_slabs.at[ia], loc.at[1]),
        pltpu.make_async_copy(ask_i.at[0], all_i.at[ia], loc.at[2]),
        pltpu.make_async_copy(ask_j.at[0], all_j.at[ja], loc.at[3]),
    ]
    for c in locals_:
        c.start()
    enter(n_ia, n_ja, ia, ja)
    rows = [
        remote(slabs, row_slabs.at[ja], row_s.at[k], row_r.at[k], (ia, lax.rem(ja + k, n_ja)))
        for k in range(1, n_ja)
    ]
    cols = [
        remote(slabs, col_slabs.at[ia], col_s.at[k], col_r.at[k],
               (lax.rem(ia + 2 * k, n_ia), ja))
        for k in range(1, half)
    ]
    own = remote(slabs, col_slabs.at[ia], fwd_s.at[0], fwd_r.at[0], (partner, ja))
    asks = [
        remote(ask_i.at[0], all_i.at[ia], ai_s.at[k], ai_r.at[k], (lax.rem(ia + k, n_ia), ja))
        for k in range(1, n_ia)
    ] + [
        remote(ask_j.at[0], all_j.at[ja], aj_s.at[k], aj_r.at[k], (ia, lax.rem(ja + k, n_ja)))
        for k in range(1, n_ja)
    ]
    for c in cols + rows + [own] + asks:
        c.start()
    forwards = [own]
    for k in range(1, half):
        source = lax.rem(ia + n_ia - 2 * k, n_ia)
        cols[k - 1].wait_recv()
        f = remote(col_slabs.at[source], col_slabs.at[source], fwd_s.at[k], fwd_r.at[k],
                   (partner, ja))
        f.start()
        forwards.append(f)
    for c in locals_:
        c.wait()
    for c in rows + forwards:
        c.wait_recv()

    def project(p, carry):
        f, s, d0, d1 = first[p], second[p], dom[p, 0], dom[p, 1]
        both = jnp.concatenate(
            [
                jnp.concatenate([row_slabs[f, d0], row_slabs[f, d1]], axis=0),
                jnp.concatenate([col_slabs[s, d0], col_slabs[s, d1]], axis=0),
            ],
            axis=1,
        )
        projected = matmul(coef[p], both, 0, 0).astype(BF16)
        aux = projected.shape[1] // 2
        exch[p] = matmul(projected[:, :aux], projected[:, aux:], 1, 1)
        return carry

    lax.fori_loop(0, coef.shape[0], project, 0)
    for c in asks:
        c.wait_recv()
    for c in rows + cols + forwards + asks:
        c.wait_send()


def amplitude_kernel(
    n_ia, n_ja, factor,
    exch, energy, shift, coef, margin_i, margin_j, cpl_i, cpl_j, link_i, link_j, all_i, all_j,
    dom,
    amp, dens,
    sent, mi, mj, acc, stage_i, stage_j, tables_i, tables_j, mf, cf, own, out1, in1, out2, in2,
    m_sem, is_, ir_, js_, jr_, s1, r1, s2, r2,
):
    ia, ja = lax.axis_index("ia"), lax.axis_index("ja")
    pairs = exch.shape[0]
    slots_i, slots_j = all_i.shape[2], all_j.shape[2]
    loads = [
        pltpu.make_async_copy(margin_j, mj, m_sem.at[0]),
        pltpu.make_async_copy(margin_i, mi, m_sem.at[1]),
    ]
    for c in loads:
        c.start()

    def denominator(p):
        e = jnp.broadcast_to(energy[pl.ds(p, 1), :], exch.shape[1:])
        return e + e.T + shift[p]

    def begin(p, carry):
        sent[p] = (-exch[p] / denominator(p)).astype(BF16)
        return carry

    lax.fori_loop(0, pairs, begin, 0)
    enter(n_ia, n_ja, ia, ja)

    def couple(p, table, margin, weights, link, total):
        for n in range(0, margin.shape[1], 2):
            sides, margins = [], []
            for m in (n, n + 1):
                block = margin[p, m]
                left = matmul(block, table[link[p, m]], 1, 0)
                sides.append((left * weights[p, m]).astype(BF16))
                margins.append(block)
            part = matmul(
                jnp.concatenate(sides, axis=1), jnp.concatenate(margins, axis=1), 1, 1
            )
            total = part if total is None else total + part
        return total

    for it in range(ITERS):
        copies_i, copies_j = [], []
        table_i, table_j = tables_i[it], tables_j[it]
        for k in range(1, n_ja):
            peer = lax.rem(ja + k, n_ja)
            for slot in range(slots_j):
                stage_j[it, k, slot] = sent[all_j[peer, ja, slot]]
            c = remote(stage_j.at[it, k], table_j.at[pl.ds(ja * slots_j, slots_j)],
                       js_.at[it, k], jr_.at[it, k], (ia, peer))
            c.start()
            copies_j.append(c)
        for k in range(1, n_ia):
            peer = lax.rem(ia + k, n_ia)
            for slot in range(slots_i):
                stage_i[it, k, slot] = sent[all_i[peer, ia, slot]]
            c = remote(stage_i.at[it, k], table_i.at[pl.ds(ia * slots_i, slots_i)],
                       is_.at[it, k], ir_.at[it, k], (peer, ja))
            c.start()
            copies_i.append(c)
        for slot in range(slots_j):
            table_j[ja * slots_j + slot] = sent[all_j[ja, ja, slot]]
        for slot in range(slots_i):
            table_i[ia * slots_i + slot] = sent[all_i[ia, ia, slot]]
        if it == 0:
            loads[0].wait()
        for c in copies_j:
            c.wait_recv()

        def second_kind(p, carry, table_j=table_j):
            acc[p] = couple(p, table_j, mj, cpl_j, link_j, None)
            return carry

        lax.fori_loop(0, pairs, second_kind, 0)
        if it == 0:
            loads[1].wait()
        for c in copies_i:
            c.wait_recv()

        def first_kind(p, carry, it=it, table_i=table_i):
            total = couple(p, table_i, mi, cpl_i, link_i, acc[p])
            new = -(exch[p] + total) / denominator(p)
            if it == ITERS - 1:
                amp[p] = new
            sent[p] = new.astype(BF16)
            return carry

        lax.fori_loop(0, pairs, first_kind, 0)
        for c in copies_i + copies_j:
            c.wait_send()

    blocks = mf.shape[1] // BLK

    def spread(p, carry):
        s = sent[p]
        square = (matmul(s, s, 1, 1) + matmul(s, s, 0, 0)).astype(BF16)
        c = coef[p]
        mapped = matmul(c, square, 1, 0).astype(BF16)
        d0, d1 = dom[p, 0], dom[p, 1]
        for b in range(blocks):
            k0 = jnp.where(d0 == b, 1.0, 0.0).astype(F32)
            k1 = jnp.where(d1 == b, 1.0, 0.0).astype(F32)
            where = pl.ds(b * BLK, BLK)
            mf[p, where] = (
                mapped[:BLK].astype(F32) * k0 + mapped[BLK:].astype(F32) * k1
            ).astype(BF16)
            cf[p, where] = (c[:BLK].astype(F32) * k0 + c[BLK:].astype(F32) * k1).astype(BF16)
        return carry

    lax.fori_loop(0, pairs, spread, 0)
    chunk = own.shape[0]

    def partial_rows(peer):
        start = pl.multiple_of(peer * chunk, chunk)
        total = None
        for p in range(0, pairs, 2):
            a = jnp.concatenate([mf[p, pl.ds(start, chunk)], mf[p + 1, pl.ds(start, chunk)]], 1)
            b = jnp.concatenate([cf[p], cf[p + 1]], 1)
            part = matmul(a, b, 1, 1)
            total = part if total is None else total + part
        return total

    sends = []
    for k in range(1, n_ia):
        peer = lax.rem(ia + k, n_ia)
        out1[k] = partial_rows(peer).astype(BF16)
        c = remote(out1.at[k], in1.at[k], s1.at[k], r1.at[k], (peer, ja))
        c.start()
        sends.append(c)
    own[...] = partial_rows(ia)
    for k in range(1, n_ia):
        sends[k - 1].wait_recv()
        own[...] += in1[k].astype(F32)
    piece = dens.shape[0]
    for j in range(n_ja):
        out2[j] = own[pl.ds(j * piece, piece), :]
    last = []
    for k in range(1, n_ja):
        peer = lax.rem(ja + k, n_ja)
        c = remote(out2.at[peer], in2.at[k], s2.at[k], r2.at[k], (ia, peer))
        c.start()
        last.append(c)
    total = out2[ja]
    for k in range(1, n_ja):
        last[k - 1].wait_recv()
        total = total + in2[k]
    dens[...] = total * factor
    for c in sends + last:
        c.wait_send()


def body(
    slabs, pno_coef, dom_blocks, pair_first, pair_second, pno_energy, pair_shift,
    margin_i, margin_j, couple_i, couple_j, ask_i, ask_j, link_i, link_j,
):
    n_ia, n_ja = lax.axis_size("ia"), lax.axis_size("ja")
    devices = n_ia * n_ja
    pairs, domain, pno = pno_coef.shape
    pao, aux = slabs.shape[1:]
    blocks = pao // BLK
    slots_i, slots_j = ask_i.shape[2], ask_j.shape[2]
    links_i, links_j = margin_i.shape[1], margin_j.shape[1]
    vmem = pl.BlockSpec(memory_space=pltpu.VMEM)
    smem = pl.BlockSpec(memory_space=pltpu.SMEM)
    anym = pl.BlockSpec(memory_space=pl.ANY)
    hbm = pl.BlockSpec(memory_space=pltpu.HBM)
    dma = pltpu.SemaphoreType.DMA
    exch, all_i, all_j = pl.pallas_call(
        functools.partial(exchange_kernel, n_ia, n_ja),
        out_shape=(
            jax.ShapeDtypeStruct((pairs, pno, pno), F32),
            jax.ShapeDtypeStruct((n_ia,) + ask_i.shape[1:], jnp.int32),
            jax.ShapeDtypeStruct((n_ja,) + ask_j.shape[1:], jnp.int32),
        ),
        in_specs=[hbm, hbm, hbm, vmem, smem, smem, smem],
        out_specs=(vmem, hbm, hbm),
        scratch_shapes=[
            pltpu.VMEM((n_ja, blocks, BLK, aux), BF16),
            pltpu.VMEM((n_ia, blocks, BLK, aux), BF16),
            dma((4,)),
            dma((n_ja,)), dma((n_ja,)),
            dma((n_ia,)), dma((n_ia,)),
            dma((n_ia,)), dma((n_ia,)),
            dma((n_ia,)), dma((n_ia,)),
            dma((n_ja,)), dma((n_ja,)),
        ],
        compiler_params=pltpu.CompilerParams(collective_id=0, has_side_effects=True),
        name="exchange",
    )(slabs.reshape(blocks, BLK, aux), ask_i, ask_j, pno_coef, dom_blocks, pair_first,
      pair_second)
    factor = 1.0 / math.sqrt(pairs * devices)
    chunk, piece = pao // n_ia, pao // devices
    return pl.pallas_call(
        functools.partial(amplitude_kernel, n_ia, n_ja, factor),
        out_shape=(
            jax.ShapeDtypeStruct((pairs, pno, pno), F32),
            jax.ShapeDtypeStruct((piece, pao), F32),
        ),
        in_specs=[vmem, vmem, smem, vmem, hbm, hbm, smem, smem, smem, smem, smem, smem, smem],
        out_specs=(vmem, vmem),
        scratch_shapes=[
            pltpu.VMEM((pairs, pno, pno), BF16),
            pltpu.VMEM((pairs, links_i, pno, pno), BF16),
            pltpu.VMEM((pairs, links_j, pno, pno), BF16),
            pltpu.VMEM((pairs, pno, pno), F32),
            pltpu.VMEM((ITERS, n_ia, slots_i, pno, pno), BF16),
            pltpu.VMEM((ITERS, n_ja, slots_j, pno, pno), BF16),
            [pltpu.VMEM((n_ia * slots_i, pno, pno), BF16)] * ITERS,
            [pltpu.VMEM((n_ja * slots_j, pno, pno), BF16)] * ITERS,
            pltpu.VMEM((pairs, pao, pno), BF16),
            pltpu.VMEM((pairs, pao, pno), BF16),
            pltpu.VMEM((chunk, pao), F32),
            pltpu.VMEM((n_ia, chunk, pao), BF16),
            pltpu.VMEM((n_ia, chunk, pao), BF16),
            pltpu.VMEM((n_ja, piece, pao), F32),
            pltpu.VMEM((n_ja, piece, pao), F32),
            dma((2,)),
            dma((ITERS, n_ia)), dma((ITERS, n_ia)),
            dma((ITERS, n_ja)), dma((ITERS, n_ja)),
            dma((n_ia,)), dma((n_ia,)),
            dma((n_ja,)), dma((n_ja,)),
        ],
        compiler_params=pltpu.CompilerParams(collective_id=1, has_side_effects=True),
        name="amplitudes",
    )(exch, pno_energy, pair_shift, pno_coef, margin_i, margin_j, couple_i, couple_j,
      link_i, link_j, all_i, all_j, dom_blocks)


def solution(mesh):
    both = ("ia", "ja")
    in_specs = (
        P(both, None, None), P(both, None, None), P(both, None), P(both), P(both),
        P(both, None), P(both), P(both, None, None, None), P(both, None, None, None),
        P(both, None), P(both, None), P(both, None, None), P(both, None, None),
        P(both, None), P(both, None),
    )
    out_specs = (P(both, None, None), P(both, None))
    return jax.shard_map(body, mesh=mesh, in_specs=in_specs, out_specs=out_specs, check_vma=False)
```

```python
import functools
import math

import jax
import jax.numpy as jnp
from jax import lax
from jax.experimental import pallas as pl
from jax.experimental.pallas import tpu as pltpu
from jax.sharding import PartitionSpec as P

BLK = 128
ITERS = 2
MESH = pl.DeviceIdType.MESH
F32 = jnp.float32
BF16 = jnp.bfloat16


def matmul(a, b, da, db):
    return lax.dot_general(a, b, (((da,), (db,)), ((), ())), preferred_element_type=F32)


def enter(n_ia, n_ja, ia, ja):
    barrier = pltpu.get_barrier_semaphore()
    for k in range(1, n_ia):
        pl.semaphore_signal(
            barrier, inc=1, device_id=(lax.rem(ia + k, n_ia), ja), device_id_type=MESH
        )
    for k in range(1, n_ja):
        pl.semaphore_signal(
            barrier, inc=1, device_id=(ia, lax.rem(ja + k, n_ja)), device_id_type=MESH
        )
    pl.semaphore_wait(barrier, n_ia + n_ja - 2)


def remote(src, dst, send, recv, device):
    return pltpu.make_async_remote_copy(
        src_ref=src, dst_ref=dst, send_sem=send, recv_sem=recv, device_id=device,
        device_id_type=MESH,
    )


def exchange_kernel(
    n_ia, n_ja,
    slabs, ask_i, ask_j, coef, dom, first, second,
    exch, all_i, all_j,
    row_slabs, col_slabs, proj,
    loc, up_s, up_r, dn_s, dn_r, col_s, col_r, fwd_s, fwd_r, ai_s, ai_r, aj_s, aj_r,
):
    ia, ja = lax.axis_index("ia"), lax.axis_index("ja")
    half = n_ia // 2
    partner = ia + 1 - 2 * lax.rem(ia, 2)
    locals_ = [
        pltpu.make_async_copy(slabs, row_slabs.at[ja], loc.at[0]),
        pltpu.make_async_copy(slabs, col_slabs.at[ia], loc.at[1]),
        pltpu.make_async_copy(ask_i.at[0], all_i.at[ia], loc.at[2]),
        pltpu.make_async_copy(ask_j.at[0], all_j.at[ja], loc.at[3]),
    ]
    for c in locals_:
        c.start()
    enter(n_ia, n_ja, ia, ja)
    blocks = slabs.shape[0]

    def up(t, c):
        at = ja - t
        src = slabs.at[c] if t == 0 else row_slabs.at[at, c]
        return remote(src, row_slabs.at[at, c], up_s.at[t, c], up_r.at[t, c], (ia, ja + 1))

    def down(t, c):
        at = ja + t
        src = slabs.at[c] if t == 0 else row_slabs.at[at, c]
        return remote(src, row_slabs.at[at, c], dn_s.at[t, c], dn_r.at[t, c], (ia, ja - 1))

    def send_rows(t, c, act):
        @pl.when((ja + 1 < n_ja) & (ja - t >= 0))
        def _():
            act(up(t, c))

        @pl.when((ja >= 1) & (ja + t < n_ja))
        def _():
            act(down(t, c))

    def take_rows(t, c):
        @pl.when(ja - 1 - t >= 0)
        def _():
            pltpu.make_async_copy(
                slabs.at[c], row_slabs.at[ja - 1 - t, c], up_r.at[t, c]
            ).wait()

        @pl.when(ja + 1 + t < n_ja)
        def _():
            pltpu.make_async_copy(
                slabs.at[c], row_slabs.at[ja + 1 + t, c], dn_r.at[t, c]
            ).wait()

    cols = [
        remote(slabs, col_slabs.at[ia], col_s.at[k], col_r.at[k],
               (lax.rem(ia + 2 * k, n_ia), ja))
        for k in range(1, half)
    ]
    own = remote(slabs, col_slabs.at[ia], fwd_s.at[0], fwd_r.at[0], (partner, ja))
    asks = [
        remote(ask_i.at[0], all_i.at[ia], ai_s.at[k], ai_r.at[k], (lax.rem(ia + k, n_ia), ja))
        for k in range(1, n_ia)
    ] + [
        remote(ask_j.at[0], all_j.at[ja], aj_s.at[k], aj_r.at[k], (ia, lax.rem(ja + k, n_ja)))
        for k in range(1, n_ja)
    ]
    for c in range(blocks):
        send_rows(0, c, lambda copy: copy.start())
    for c in cols + [own] + asks:
        c.start()
    for t in range(n_ja - 2):
        for c in range(blocks):
            take_rows(t, c)
            send_rows(t + 1, c, lambda copy: copy.start())
    forwards = [own]
    for k in range(1, half):
        source = lax.rem(ia + n_ia - 2 * k, n_ia)
        cols[k - 1].wait_recv()
        f = remote(col_slabs.at[source], col_slabs.at[source], fwd_s.at[k], fwd_r.at[k],
                   (partner, ja))
        f.start()
        forwards.append(f)
    for c in locals_:
        c.wait()
    for c in forwards:
        c.wait_recv()

    def gathered(table, o, p):
        return jnp.concatenate([table[o, dom[0, p]], table[o, dom[1, p]]], axis=0)

    def project_second(p, carry):
        proj[p] = matmul(coef[p], gathered(col_slabs, second[p], p), 0, 0).astype(BF16)
        return carry

    lax.fori_loop(0, coef.shape[0], project_second, 0)
    for c in range(blocks):
        take_rows(n_ja - 2, c)

    def project_first(p, carry):
        projected = matmul(coef[p], gathered(row_slabs, first[p], p), 0, 0).astype(BF16)
        exch[p] = matmul(projected, proj[p], 1, 1)
        return carry

    lax.fori_loop(0, coef.shape[0], project_first, 0)
    for c in asks:
        c.wait_recv()
    for t in range(n_ja - 1):
        for c in range(blocks):
            send_rows(t, c, lambda copy: copy.wait_send())
    for c in cols + forwards + asks:
        c.wait_send()


def amplitude_kernel(
    n_ia, n_ja, factor,
    exch, energy, shift, coef, margin_i, margin_j, cpl_i, cpl_j, link_i, link_j, all_i, all_j,
    dom,
    amp, dens,
    sent, mi, mj, acc, stage_i, stage_j, tables_i, tables_j, mf, cf, own, out1, in1, out2, in2,
    m_sem, is_, ir_, js_, jr_, s1, r1, s2, r2,
):
    ia, ja = lax.axis_index("ia"), lax.axis_index("ja")
    pairs = exch.shape[0]
    slots_i, slots_j = all_i.shape[1], all_j.shape[2]
    loads = [
        pltpu.make_async_copy(margin_j, mj, m_sem.at[0]),
        pltpu.make_async_copy(margin_i, mi, m_sem.at[1]),
    ]
    for c in loads:
        c.start()

    def denominator(p):
        e = jnp.broadcast_to(energy[pl.ds(p, 1), :], exch.shape[1:])
        return e + e.T + shift[p]

    def begin(p, carry):
        sent[p] = (-exch[p] / denominator(p)).astype(BF16)
        return carry

    lax.fori_loop(0, pairs, begin, 0)
    enter(n_ia, n_ja, ia, ja)

    def couple(p, table, margin, weights, link, total):
        for n in range(0, margin.shape[1], 2):
            sides, margins = [], []
            for m in (n, n + 1):
                block = margin[p, m]
                left = matmul(block, table[link[p, m]], 1, 0)
                sides.append((left * weights[p, m]).astype(BF16))
                margins.append(block)
            part = matmul(
                jnp.concatenate(sides, axis=1), jnp.concatenate(margins, axis=1), 1, 1
            )
            total = part if total is None else total + part
        return total

    for it in range(ITERS):
        copies_i, copies_j = [], []
        table_i, table_j = tables_i[it], tables_j[it]
        for k in range(1, n_ja):
            peer = lax.rem(ja + k, n_ja)
            for slot in range(slots_j):
                stage_j[it, k, slot] = sent[all_j[peer, ja, slot]]
            c = remote(stage_j.at[it, k], table_j.at[pl.ds(ja * slots_j, slots_j)],
                       js_.at[it, k], jr_.at[it, k], (ia, peer))
            c.start()
            copies_j.append(c)
        for k in range(1, n_ia):
            peer = lax.rem(ia + k, n_ia)
            for slot in range(slots_i):
                stage_i[it, k, slot] = sent[all_i[peer, slot, ia]]
            c = remote(stage_i.at[it, k], table_i.at[pl.ds(ia * slots_i, slots_i)],
                       is_.at[it, k], ir_.at[it, k], (peer, ja))
            c.start()
            copies_i.append(c)
        for slot in range(slots_j):
            table_j[ja * slots_j + slot] = sent[all_j[ja, ja, slot]]
        for slot in range(slots_i):
            table_i[ia * slots_i + slot] = sent[all_i[ia, slot, ia]]
        if it == 0:
            loads[0].wait()
        for c in copies_j:
            c.wait_recv()

        def second_kind(p, carry, table_j=table_j):
            acc[p] = couple(p, table_j, mj, cpl_j, link_j, None)
            return carry

        lax.fori_loop(0, pairs, second_kind, 0)
        if it == 0:
            loads[1].wait()
        for c in copies_i:
            c.wait_recv()

        def first_kind(p, carry, it=it, table_i=table_i):
            total = couple(p, table_i, mi, cpl_i, link_i, acc[p])
            new = -(exch[p] + total) / denominator(p)
            if it == ITERS - 1:
                amp[p] = new
            sent[p] = new.astype(BF16)
            return carry

        lax.fori_loop(0, pairs, first_kind, 0)
        for c in copies_i + copies_j:
            c.wait_send()

    blocks = mf.shape[1] // BLK

    def spread(p, carry):
        s = sent[p]
        square = (matmul(s, s, 1, 1) + matmul(s, s, 0, 0)).astype(BF16)
        c = coef[p]
        mapped = matmul(c, square, 1, 0).astype(BF16)
        d0, d1 = dom[0, p], dom[1, p]
        for b in range(blocks):
            k0 = jnp.where(d0 == b, 1.0, 0.0).astype(F32)
            k1 = jnp.where(d1 == b, 1.0, 0.0).astype(F32)
            where = pl.ds(b * BLK, BLK)
            mf[p, where] = (
                mapped[:BLK].astype(F32) * k0 + mapped[BLK:].astype(F32) * k1
            ).astype(BF16)
            cf[p, where] = (c[:BLK].astype(F32) * k0 + c[BLK:].astype(F32) * k1).astype(BF16)
        return carry

    lax.fori_loop(0, pairs, spread, 0)
    chunk = own.shape[0]

    def partial_rows(peer):
        start = pl.multiple_of(peer * chunk, chunk)
        total = None
        for p in range(0, pairs, 2):
            a = jnp.concatenate([mf[p, pl.ds(start, chunk)], mf[p + 1, pl.ds(start, chunk)]], 1)
            b = jnp.concatenate([cf[p], cf[p + 1]], 1)
            part = matmul(a, b, 1, 1)
            total = part if total is None else total + part
        return total

    sends = []
    for k in range(1, n_ia):
        peer = lax.rem(ia + k, n_ia)
        out1[k] = partial_rows(peer).astype(BF16)
        c = remote(out1.at[k], in1.at[k], s1.at[k], r1.at[k], (peer, ja))
        c.start()
        sends.append(c)
    own[...] = partial_rows(ia)
    for k in range(1, n_ia):
        sends[k - 1].wait_recv()
        own[...] += in1[k].astype(F32)
    piece = dens.shape[0]
    for j in range(n_ja):
        out2[j] = own[pl.ds(j * piece, piece), :]
    last = []
    for k in range(1, n_ja):
        peer = lax.rem(ja + k, n_ja)
        c = remote(out2.at[peer], in2.at[k], s2.at[k], r2.at[k], (ia, peer))
        c.start()
        last.append(c)
    total = out2[ja]
    for k in range(1, n_ja):
        last[k - 1].wait_recv()
        total = total + in2[k]
    dens[...] = total * factor
    for c in sends + last:
        c.wait_send()


def body(
    slabs, pno_coef, dom_blocks, pair_first, pair_second, pno_energy, pair_shift,
    margin_i, margin_j, couple_i, couple_j, ask_i, ask_j, link_i, link_j,
):
    n_ia, n_ja = lax.axis_size("ia"), lax.axis_size("ja")
    devices = n_ia * n_ja
    pairs, domain, pno = pno_coef.shape
    pao, aux = slabs.shape[1:]
    blocks = pao // BLK
    slots_i, slots_j = ask_i.shape[2], ask_j.shape[2]
    links_i, links_j = margin_i.shape[1], margin_j.shape[1]
    ask_i = ask_i.transpose(0, 2, 1)
    dom_blocks = dom_blocks.T
    vmem = pl.BlockSpec(memory_space=pltpu.VMEM)
    smem = pl.BlockSpec(memory_space=pltpu.SMEM)
    anym = pl.BlockSpec(memory_space=pl.ANY)
    hbm = pl.BlockSpec(memory_space=pltpu.HBM)
    dma = pltpu.SemaphoreType.DMA
    exch, all_i, all_j = pl.pallas_call(
        functools.partial(exchange_kernel, n_ia, n_ja),
        out_shape=(
            jax.ShapeDtypeStruct((pairs, pno, pno), F32),
            jax.ShapeDtypeStruct((n_ia,) + ask_i.shape[1:], jnp.int32),
            jax.ShapeDtypeStruct((n_ja,) + ask_j.shape[1:], jnp.int32),
        ),
        in_specs=[hbm, hbm, hbm, vmem, smem, smem, smem],
        out_specs=(vmem, hbm, hbm),
        scratch_shapes=[
            pltpu.VMEM((n_ja, blocks, BLK, aux), BF16),
            pltpu.VMEM((n_ia, blocks, BLK, aux), BF16),
            pltpu.VMEM((pairs, pno, aux), BF16),
            dma((4,)),
            dma((n_ja, blocks)), dma((n_ja, blocks)),
            dma((n_ja, blocks)), dma((n_ja, blocks)),
            dma((n_ia,)), dma((n_ia,)),
            dma((n_ia,)), dma((n_ia,)),
            dma((n_ia,)), dma((n_ia,)),
            dma((n_ja,)), dma((n_ja,)),
        ],
        compiler_params=pltpu.CompilerParams(collective_id=0, has_side_effects=True),
        name="exchange",
    )(slabs.reshape(blocks, BLK, aux), ask_i, ask_j, pno_coef, dom_blocks, pair_first,
      pair_second)
    factor = 1.0 / math.sqrt(pairs * devices)
    chunk, piece = pao // n_ia, pao // devices
    return pl.pallas_call(
        functools.partial(amplitude_kernel, n_ia, n_ja, factor),
        out_shape=(
            jax.ShapeDtypeStruct((pairs, pno, pno), F32),
            jax.ShapeDtypeStruct((piece, pao), F32),
        ),
        in_specs=[vmem, vmem, smem, vmem, hbm, hbm, smem, smem, smem, smem, smem, smem, smem],
        out_specs=(vmem, vmem),
        scratch_shapes=[
            pltpu.VMEM((pairs, pno, pno), BF16),
            pltpu.VMEM((pairs, links_i, pno, pno), BF16),
            pltpu.VMEM((pairs, links_j, pno, pno), BF16),
            pltpu.VMEM((pairs, pno, pno), F32),
            pltpu.VMEM((ITERS, n_ia, slots_i, pno, pno), BF16),
            pltpu.VMEM((ITERS, n_ja, slots_j, pno, pno), BF16),
            [pltpu.VMEM((n_ia * slots_i, pno, pno), BF16)] * ITERS,
            [pltpu.VMEM((n_ja * slots_j, pno, pno), BF16)] * ITERS,
            pltpu.VMEM((pairs, pao, pno), BF16),
            pltpu.VMEM((pairs, pao, pno), BF16),
            pltpu.VMEM((chunk, pao), F32),
            pltpu.VMEM((n_ia, chunk, pao), BF16),
            pltpu.VMEM((n_ia, chunk, pao), BF16),
            pltpu.VMEM((n_ja, piece, pao), F32),
            pltpu.VMEM((n_ja, piece, pao), F32),
            dma((2,)),
            dma((ITERS, n_ia)), dma((ITERS, n_ia)),
            dma((ITERS, n_ja)), dma((ITERS, n_ja)),
            dma((n_ia,)), dma((n_ia,)),
            dma((n_ja,)), dma((n_ja,)),
        ],
        compiler_params=pltpu.CompilerParams(collective_id=1, has_side_effects=True),
        name="amplitudes",
    )(exch, pno_energy, pair_shift, pno_coef, margin_i, margin_j, couple_i, couple_j,
      link_i, link_j, all_i, all_j, dom_blocks)


def solution(mesh):
    both = ("ia", "ja")
    in_specs = (
        P(both, None, None), P(both, None, None), P(both, None), P(both), P(both),
        P(both, None), P(both), P(both, None, None, None), P(both, None, None, None),
        P(both, None), P(both, None), P(both, None, None), P(both, None, None),
        P(both, None), P(both, None),
    )
    out_specs = (P(both, None, None), P(both, None))
    return jax.shard_map(body, mesh=mesh, in_specs=in_specs, out_specs=out_specs, check_vma=False)
```

```python
import functools
import math

import jax
import jax.numpy as jnp
from jax import lax
from jax.experimental import pallas as pl
from jax.experimental.pallas import tpu as pltpu
from jax.sharding import PartitionSpec as P

BLK = 128
ITERS = 2
MESH = pl.DeviceIdType.MESH
F32 = jnp.float32
BF16 = jnp.bfloat16


def matmul(a, b, da, db):
    return lax.dot_general(a, b, (((da,), (db,)), ((), ())), preferred_element_type=F32)


def enter(n_ia, n_ja, ia, ja):
    barrier = pltpu.get_barrier_semaphore()
    for k in range(1, n_ia):
        pl.semaphore_signal(
            barrier, inc=1, device_id=(lax.rem(ia + k, n_ia), ja), device_id_type=MESH
        )
    for k in range(1, n_ja):
        pl.semaphore_signal(
            barrier, inc=1, device_id=(ia, lax.rem(ja + k, n_ja)), device_id_type=MESH
        )
    pl.semaphore_wait(barrier, n_ia + n_ja - 2)


def remote(src, dst, send, recv, device):
    return pltpu.make_async_remote_copy(
        src_ref=src, dst_ref=dst, send_sem=send, recv_sem=recv, device_id=device,
        device_id_type=MESH,
    )


def exchange_kernel(
    n_ia, n_ja,
    slabs, ask_i, ask_j, coef, dom, first, second,
    exch, all_i, all_j,
    row_slabs, col_slabs, proj,
    loc, up_s, up_r, dn_s, dn_r, col_s, col_r, fwd_s, fwd_r, ai_s, ai_r, aj_s, aj_r,
):
    ia, ja = lax.axis_index("ia"), lax.axis_index("ja")
    half = n_ia // 2
    partner = ia + 1 - 2 * lax.rem(ia, 2)
    locals_ = [
        pltpu.make_async_copy(slabs, row_slabs.at[ja], loc.at[0]),
        pltpu.make_async_copy(slabs, col_slabs.at[ia], loc.at[1]),
        pltpu.make_async_copy(ask_i.at[0], all_i.at[ia], loc.at[2]),
        pltpu.make_async_copy(ask_j.at[0], all_j.at[ja], loc.at[3]),
    ]
    for c in locals_:
        c.start()
    enter(n_ia, n_ja, ia, ja)
    blocks = slabs.shape[0]

    def up(t, c):
        at = ja - t
        src = slabs.at[c] if t == 0 else row_slabs.at[at, c]
        return remote(src, row_slabs.at[at, c], up_s.at[t, c], up_r.at[t, c], (ia, ja + 1))

    def down(t, c):
        at = ja + t
        src = slabs.at[c] if t == 0 else row_slabs.at[at, c]
        return remote(src, row_slabs.at[at, c], dn_s.at[t, c], dn_r.at[t, c], (ia, ja - 1))

    def send_rows(t, c, act):
        @pl.when((ja + 1 < n_ja) & (ja - t >= 0))
        def _():
            act(up(t, c))

        @pl.when((ja >= 1) & (ja + t < n_ja))
        def _():
            act(down(t, c))

    def take_rows(t, c):
        @pl.when(ja - 1 - t >= 0)
        def _():
            pltpu.make_async_copy(
                slabs.at[c], row_slabs.at[ja - 1 - t, c], up_r.at[t, c]
            ).wait()

        @pl.when(ja + 1 + t < n_ja)
        def _():
            pltpu.make_async_copy(
                slabs.at[c], row_slabs.at[ja + 1 + t, c], dn_r.at[t, c]
            ).wait()

    cols = [
        remote(slabs, col_slabs.at[ia], col_s.at[k], col_r.at[k],
               (lax.rem(ia + 2 * k, n_ia), ja))
        for k in range(1, half)
    ]
    own = remote(slabs, col_slabs.at[ia], fwd_s.at[0], fwd_r.at[0], (partner, ja))
    asks = [
        remote(ask_i.at[0], all_i.at[ia], ai_s.at[k], ai_r.at[k], (lax.rem(ia + k, n_ia), ja))
        for k in range(1, n_ia)
    ] + [
        remote(ask_j.at[0], all_j.at[ja], aj_s.at[k], aj_r.at[k], (ia, lax.rem(ja + k, n_ja)))
        for k in range(1, n_ja)
    ]
    for c in range(blocks):
        send_rows(0, c, lambda copy: copy.start())
    for c in cols + [own] + asks:
        c.start()
    for t in range(n_ja - 2):
        for c in range(blocks):
            take_rows(t, c)
            send_rows(t + 1, c, lambda copy: copy.start())
    forwards = [own]
    for k in range(1, half):
        source = lax.rem(ia + n_ia - 2 * k, n_ia)
        cols[k - 1].wait_recv()
        f = remote(col_slabs.at[source], col_slabs.at[source], fwd_s.at[k], fwd_r.at[k],
                   (partner, ja))
        f.start()
        forwards.append(f)
    for c in locals_:
        c.wait()
    for c in forwards:
        c.wait_recv()

    def gathered(table, o, p):
        return jnp.concatenate([table[o, dom[0, p]], table[o, dom[1, p]]], axis=0)

    def project_second(p, carry):
        proj[p] = matmul(coef[p], gathered(col_slabs, second[p], p), 0, 0).astype(BF16)
        return carry

    lax.fori_loop(0, coef.shape[0], project_second, 0)
    for c in range(blocks):
        take_rows(n_ja - 2, c)

    def project_first(p, carry):
        projected = matmul(coef[p], gathered(row_slabs, first[p], p), 0, 0).astype(BF16)
        exch[p] = matmul(projected, proj[p], 1, 1)
        return carry

    lax.fori_loop(0, coef.shape[0], project_first, 0, unroll=4)
    for c in asks:
        c.wait_recv()
    for t in range(n_ja - 1):
        for c in range(blocks):
            send_rows(t, c, lambda copy: copy.wait_send())
    for c in cols + forwards + asks:
        c.wait_send()


def amplitude_kernel(
    n_ia, n_ja, factor,
    exch, energy, shift, coef, margin_i, margin_j, cpl_i, cpl_j, link_i, link_j, all_i, all_j,
    dom,
    amp, dens,
    sent, mi, mj, acc, stage_i, stage_j, tables_i, tables_j, mf, cf, own, out1, in1, out2, in2,
    m_sem, is_, ir_, js_, jr_, s1, r1, s2, r2,
):
    ia, ja = lax.axis_index("ia"), lax.axis_index("ja")
    pairs = exch.shape[0]
    slots_i, slots_j = all_i.shape[1], all_j.shape[2]
    loads = [
        pltpu.make_async_copy(margin_j, mj, m_sem.at[0]),
        pltpu.make_async_copy(margin_i, mi, m_sem.at[1]),
    ]
    for c in loads:
        c.start()

    def denominator(p):
        e = jnp.broadcast_to(energy[pl.ds(p, 1), :], exch.shape[1:])
        return e + e.T + shift[p]

    def begin(p, carry):
        sent[p] = (-exch[p] / denominator(p)).astype(BF16)
        return carry

    lax.fori_loop(0, pairs, begin, 0)
    enter(n_ia, n_ja, ia, ja)

    def couple(p, table, margin, weights, link, total):
        for n in range(0, margin.shape[1], 2):
            sides, margins = [], []
            for m in (n, n + 1):
                block = margin[p, m]
                left = matmul(block, table[link[p, m]], 1, 0)
                sides.append((left * weights[p, m]).astype(BF16))
                margins.append(block)
            part = matmul(
                jnp.concatenate(sides, axis=1), jnp.concatenate(margins, axis=1), 1, 1
            )
            total = part if total is None else total + part
        return total

    for it in range(ITERS):
        copies_i, copies_j = [], []
        table_i, table_j = tables_i[it], tables_j[it]
        for k in range(1, n_ja):
            peer = lax.rem(ja + k, n_ja)
            for slot in range(slots_j):
                stage_j[it, k, slot] = sent[all_j[peer, ja, slot]]
            c = remote(stage_j.at[it, k], table_j.at[pl.ds(ja * slots_j, slots_j)],
                       js_.at[it, k], jr_.at[it, k], (ia, peer))
            c.start()
            copies_j.append(c)
        for k in range(1, n_ia):
            peer = lax.rem(ia + k, n_ia)
            for slot in range(slots_i):
                stage_i[it, k, slot] = sent[all_i[peer, slot, ia]]
            c = remote(stage_i.at[it, k], table_i.at[pl.ds(ia * slots_i, slots_i)],
                       is_.at[it, k], ir_.at[it, k], (peer, ja))
            c.start()
            copies_i.append(c)
        for slot in range(slots_j):
            table_j[ja * slots_j + slot] = sent[all_j[ja, ja, slot]]
        for slot in range(slots_i):
            table_i[ia * slots_i + slot] = sent[all_i[ia, slot, ia]]
        if it == 0:
            loads[0].wait()
        for c in copies_j:
            c.wait_recv()

        def second_kind(p, carry, table_j=table_j):
            acc[p] = couple(p, table_j, mj, cpl_j, link_j, None)
            return carry

        lax.fori_loop(0, pairs, second_kind, 0, unroll=4)
        if it == 0:
            loads[1].wait()
        for c in copies_i:
            c.wait_recv()

        def first_kind(p, carry, it=it, table_i=table_i):
            total = couple(p, table_i, mi, cpl_i, link_i, acc[p])
            new = -(exch[p] + total) / denominator(p)
            if it == ITERS - 1:
                amp[p] = new
            sent[p] = new.astype(BF16)
            return carry

        lax.fori_loop(0, pairs, first_kind, 0, unroll=4)
        for c in copies_i + copies_j:
            c.wait_send()

    blocks = mf.shape[1] // BLK

    def spread(p, carry):
        s = sent[p]
        square = (matmul(s, s, 1, 1) + matmul(s, s, 0, 0)).astype(BF16)
        c = coef[p]
        mapped = matmul(c, square, 1, 0).astype(BF16)
        d0, d1 = dom[0, p], dom[1, p]
        for b in range(blocks):
            k0 = jnp.where(d0 == b, 1.0, 0.0).astype(F32)
            k1 = jnp.where(d1 == b, 1.0, 0.0).astype(F32)
            where = pl.ds(b * BLK, BLK)
            mf[p, where] = (
                mapped[:BLK].astype(F32) * k0 + mapped[BLK:].astype(F32) * k1
            ).astype(BF16)
            cf[p, where] = (c[:BLK].astype(F32) * k0 + c[BLK:].astype(F32) * k1).astype(BF16)
        return carry

    lax.fori_loop(0, pairs, spread, 0, unroll=4)
    chunk = own.shape[0]

    def partial_rows(peer):
        start = pl.multiple_of(peer * chunk, chunk)
        total = None
        for p in range(0, pairs, 2):
            a = jnp.concatenate([mf[p, pl.ds(start, chunk)], mf[p + 1, pl.ds(start, chunk)]], 1)
            b = jnp.concatenate([cf[p], cf[p + 1]], 1)
            part = matmul(a, b, 1, 1)
            total = part if total is None else total + part
        return total

    sends = []
    for k in range(1, n_ia):
        peer = lax.rem(ia + k, n_ia)
        out1[k] = partial_rows(peer).astype(BF16)
        c = remote(out1.at[k], in1.at[k], s1.at[k], r1.at[k], (peer, ja))
        c.start()
        sends.append(c)
    own[...] = partial_rows(ia)
    for k in range(1, n_ia):
        sends[k - 1].wait_recv()
        own[...] += in1[k].astype(F32)
    piece = dens.shape[0]
    for j in range(n_ja):
        out2[j] = own[pl.ds(j * piece, piece), :].astype(BF16)
    last = []
    for k in range(1, n_ja):
        peer = lax.rem(ja + k, n_ja)
        c = remote(out2.at[peer], in2.at[k], s2.at[k], r2.at[k], (ia, peer))
        c.start()
        last.append(c)
    total = out2[ja].astype(F32)
    for k in range(1, n_ja):
        last[k - 1].wait_recv()
        total = total + in2[k].astype(F32)
    dens[...] = total * factor
    for c in sends + last:
        c.wait_send()


def body(
    slabs, pno_coef, dom_blocks, pair_first, pair_second, pno_energy, pair_shift,
    margin_i, margin_j, couple_i, couple_j, ask_i, ask_j, link_i, link_j,
):
    n_ia, n_ja = lax.axis_size("ia"), lax.axis_size("ja")
    devices = n_ia * n_ja
    pairs, domain, pno = pno_coef.shape
    pao, aux = slabs.shape[1:]
    blocks = pao // BLK
    slots_i, slots_j = ask_i.shape[2], ask_j.shape[2]
    links_i, links_j = margin_i.shape[1], margin_j.shape[1]
    ask_i = ask_i.transpose(0, 2, 1)
    dom_blocks = dom_blocks.T
    vmem = pl.BlockSpec(memory_space=pltpu.VMEM)
    smem = pl.BlockSpec(memory_space=pltpu.SMEM)
    anym = pl.BlockSpec(memory_space=pl.ANY)
    hbm = pl.BlockSpec(memory_space=pltpu.HBM)
    dma = pltpu.SemaphoreType.DMA
    exch, all_i, all_j = pl.pallas_call(
        functools.partial(exchange_kernel, n_ia, n_ja),
        out_shape=(
            jax.ShapeDtypeStruct((pairs, pno, pno), F32),
            jax.ShapeDtypeStruct((n_ia,) + ask_i.shape[1:], jnp.int32),
            jax.ShapeDtypeStruct((n_ja,) + ask_j.shape[1:], jnp.int32),
        ),
        in_specs=[hbm, hbm, hbm, vmem, smem, smem, smem],
        out_specs=(vmem, hbm, hbm),
        scratch_shapes=[
            pltpu.VMEM((n_ja, blocks, BLK, aux), BF16),
            pltpu.VMEM((n_ia, blocks, BLK, aux), BF16),
            pltpu.VMEM((pairs, pno, aux), BF16),
            dma((4,)),
            dma((n_ja, blocks)), dma((n_ja, blocks)),
            dma((n_ja, blocks)), dma((n_ja, blocks)),
            dma((n_ia,)), dma((n_ia,)),
            dma((n_ia,)), dma((n_ia,)),
            dma((n_ia,)), dma((n_ia,)),
            dma((n_ja,)), dma((n_ja,)),
        ],
        compiler_params=pltpu.CompilerParams(collective_id=0, has_side_effects=True),
        name="exchange",
    )(slabs.reshape(blocks, BLK, aux), ask_i, ask_j, pno_coef, dom_blocks, pair_first,
      pair_second)
    factor = 1.0 / math.sqrt(pairs * devices)
    chunk, piece = pao // n_ia, pao // devices
    return pl.pallas_call(
        functools.partial(amplitude_kernel, n_ia, n_ja, factor),
        out_shape=(
            jax.ShapeDtypeStruct((pairs, pno, pno), F32),
            jax.ShapeDtypeStruct((piece, pao), F32),
        ),
        in_specs=[vmem, vmem, smem, vmem, hbm, hbm, smem, smem, smem, smem, smem, smem, smem],
        out_specs=(vmem, vmem),
        scratch_shapes=[
            pltpu.VMEM((pairs, pno, pno), BF16),
            pltpu.VMEM((pairs, links_i, pno, pno), BF16),
            pltpu.VMEM((pairs, links_j, pno, pno), BF16),
            pltpu.VMEM((pairs, pno, pno), F32),
            pltpu.VMEM((ITERS, n_ia, slots_i, pno, pno), BF16),
            pltpu.VMEM((ITERS, n_ja, slots_j, pno, pno), BF16),
            [pltpu.VMEM((n_ia * slots_i, pno, pno), BF16)] * ITERS,
            [pltpu.VMEM((n_ja * slots_j, pno, pno), BF16)] * ITERS,
            pltpu.VMEM((pairs, pao, pno), BF16),
            pltpu.VMEM((pairs, pao, pno), BF16),
            pltpu.VMEM((chunk, pao), F32),
            pltpu.VMEM((n_ia, chunk, pao), BF16),
            pltpu.VMEM((n_ia, chunk, pao), BF16),
            pltpu.VMEM((n_ja, piece, pao), BF16),
            pltpu.VMEM((n_ja, piece, pao), BF16),
            dma((2,)),
            dma((ITERS, n_ia)), dma((ITERS, n_ia)),
            dma((ITERS, n_ja)), dma((ITERS, n_ja)),
            dma((n_ia,)), dma((n_ia,)),
            dma((n_ja,)), dma((n_ja,)),
        ],
        compiler_params=pltpu.CompilerParams(collective_id=1, has_side_effects=True),
        name="amplitudes",
    )(exch, pno_energy, pair_shift, pno_coef, margin_i, margin_j, couple_i, couple_j,
      link_i, link_j, all_i, all_j, dom_blocks)


def solution(mesh):
    both = ("ia", "ja")
    in_specs = (
        P(both, None, None), P(both, None, None), P(both, None), P(both), P(both),
        P(both, None), P(both), P(both, None, None, None), P(both, None, None, None),
        P(both, None), P(both, None), P(both, None, None), P(both, None, None),
        P(both, None), P(both, None),
    )
    out_specs = (P(both, None, None), P(both, None))
    return jax.shard_map(body, mesh=mesh, in_specs=in_specs, out_specs=out_specs, check_vma=False)
```
